32 devices in a mesh: grp: 2 (over y), ti: 4 (over x, core), tj: 4 (over z).
Axes of the slice: x: 2, y: 2, z: 4, core: 2. Of those that a mesh axis runs over, the one named last changes fastest.
Arguments:
- corpus: bfloat16 [2, 24576, 1024], P('grp', ('ti', 'tj')), may hold values from -64 to 64
- slot_of_row: int32 [2, 24576], P('grp', ('ti', 'tj')), may hold values from -1 to 24575, as said below
Outputs:
- max_similarity: float32 [2, 12288], P('grp', ('ti', 'tj'))
The draws below stay inside these ranges and needn't reach their ends.
Inputs may be any that keep to these rules, and one draw needn't show every extreme that they name: `slot_of_row`: every value from 0 to 24575 appears exactly once; a row with value v lies on a device whose ti index is (v % 12288) // 3072; from one device at most 192 rows have values in one aligned group of 768 consecutive values, and some device sends exactly 192 to some group.
All inputs are finite; a program needn't handle non-finite values.
Results may differ from the reference program's by a relative error of at most 0.0009.
Values may be sent and summed in bfloat16 or wider, within the bound.
A program may use at most 64 MiB of HBM per device.

```python
import jax
import jax.numpy as jnp
from jax import lax

D = 1024
BLK = 3072
GROUPS = 2
SUB_ROWS = 768
CAP = 192
SRC_DEV = 1536
CLUSTER = 12288
GRID_ROWS = 24576


def slot_table(key):
    lane_count = BLK // SUB_ROWS
    owners = 2 * lane_count
    average = CAP // 2
    key_list = jax.random.split(jax.random.fold_in(key, 11), 4)
    swings = jax.random.randint(key_list[0], (lane_count, lane_count), -average, average + 1)
    swings = swings.at[:, 0].set(average)
    paired = jnp.stack([average + swings, average - swings], axis=2).reshape(lane_count, owners)
    orders = jax.vmap(lambda sub_key: jax.random.permutation(sub_key, owners))(jax.random.split(key_list[1], lane_count))
    shares = jnp.take_along_axis(paired, orders, axis=1)
    sender = jnp.arange(owners)
    offsets = (sender[None, :] - sender[:, None]) % owners
    counts = shares[:, offsets]
    ends = jnp.cumsum(counts, axis=2)
    starts = ends - counts
    members = jnp.arange(SUB_ROWS)
    target = jnp.sum((members[None, None, :, None] >= ends[:, :, None, :]).astype(jnp.int32), axis=3)
    within = members[None, None, :] - jnp.take_along_axis(starts, target, axis=2)
    arrival = jnp.cumsum(counts, axis=1) - counts
    position = jnp.take_along_axis(arrival, target, axis=2) + within
    shuffles = jax.vmap(lambda sub_key: jax.random.permutation(sub_key, SUB_ROWS))(jax.random.split(key_list[2], lane_count * owners))
    shuffles = shuffles.reshape(lane_count, owners * SUB_ROWS)
    lookup = (target * SUB_ROWS + position).reshape(lane_count, owners * SUB_ROWS)
    placed = jnp.take_along_axis(shuffles, lookup, axis=1).reshape(lane_count, owners, SUB_ROWS)
    row_index = jnp.arange(lane_count)[:, None, None]
    values = target // lane_count * CLUSTER + row_index * BLK + target % lane_count * SUB_ROWS + placed
    local_rows = jax.vmap(lambda sub_key: jax.random.permutation(sub_key, SRC_DEV))(jax.random.split(key_list[3], lane_count * owners))[:, :SUB_ROWS]
    table = jax.vmap(lambda spots, entries: jnp.full((SRC_DEV,), -1, jnp.int32).at[spots].set(entries.astype(jnp.int32)))(local_rows, values.reshape(lane_count * owners, SUB_ROWS))
    table = table.reshape(lane_count, 2, lane_count, SRC_DEV).transpose(1, 0, 2, 3).reshape(2, lane_count * lane_count * SRC_DEV)
    return table.astype(jnp.int32)


def draw_slot_of_row(key, part):
    return slot_table(key)


def draw_corpus(key, part):
    table = slot_table(key)
    total = 2 * CLUSTER
    key_list = jax.random.split(jax.random.fold_in(key, 23), 9)
    basis = jax.random.normal(key_list[0], (total, D), jnp.float32)
    partner = jnp.concatenate([jax.random.permutation(key_list[1], CLUSTER), CLUSTER + jax.random.permutation(key_list[2], CLUSTER)])
    strong = jax.random.randint(key_list[3], (total,), 0, 4) == 0
    mixing = jnp.where(strong, jax.random.uniform(key_list[4], (total,), jnp.float32, 1.0, 4.0), jax.random.uniform(key_list[5], (total,), jnp.float32, 0.0, 0.3))
    cluster_rows = basis + mixing[:, None] * basis[partner]
    filler = jax.random.normal(key_list[8], (2, GRID_ROWS, D), jnp.float32)
    chosen = cluster_rows[jnp.clip(table, 0, total - 1)]
    result = jnp.where((table >= 0)[..., None], chosen, filler)
    return jnp.clip(result, -64.0, 64.0).astype(jnp.bfloat16)


def setup_inputs(seed: int = 0) -> dict:
    streams_of = jax.random.split(jax.random.key(seed), 3)
    return {
        "corpus": draw_corpus(jax.random.fold_in(streams_of[2], 71), 0),
        "slot_of_row": draw_slot_of_row(jax.random.fold_in(streams_of[2], 71), 0),
    }


epsilon = 1e-06

def reference(corpus, slot_of_row):
    features = corpus.shape[2]
    flat_rows = corpus.reshape(-1, features)
    slots = slot_of_row.reshape(-1).astype(jnp.int32)
    total = GROUPS * CLUSTER
    target = jnp.where(slots >= 0, slots, total).astype(jnp.int32)
    cluster_rows = jnp.zeros((total, features), corpus.dtype).at[target].set(flat_rows, mode='drop')
    widened = cluster_rows.astype(jnp.float32)
    row_squares = lax.optimization_barrier(jnp.sum(widened * widened, axis=1, keepdims=True))
    inverse_norm = lax.rsqrt(row_squares + epsilon)
    unit_rows = (widened * inverse_norm).astype(jnp.bfloat16)
    per_group = CLUSTER // BLK

    def one_block(pair_index):
        group_start = pair_index // per_group * CLUSTER
        local_start = pair_index % per_group * BLK
        queries = lax.dynamic_slice_in_dim(unit_rows, (group_start + local_start).astype(jnp.int32), BLK, 0)
        members = lax.dynamic_slice_in_dim(unit_rows, group_start.astype(jnp.int32), CLUSTER, 0)
        scores = jnp.dot(queries, members.T, preferred_element_type=jnp.float32)
        same = (local_start + jnp.arange(BLK, dtype=jnp.int32))[:, None] == jnp.arange(CLUSTER, dtype=jnp.int32)[None, :]
        scores = jnp.where(same, -2.0, scores)
        return lax.optimization_barrier(jnp.max(scores, axis=1))
    best = lax.map(one_block, jnp.arange(GROUPS * per_group, dtype=jnp.int32))
    return best.reshape(GROUPS, CLUSTER)
```

```python
import functools

import jax
import jax.numpy as jnp
from jax import lax
from jax.experimental import pallas as pl
from jax.experimental.pallas import tpu as pltpu
from jax.sharding import PartitionSpec as P

MESH = pl.DeviceIdType.MESH
NT = (((1,), (1,)), ((), ()))
NN = (((1,), (0,)), ((), ()))
CORES = 2
EPSILON = 1e-06


def dot(a, b, dims):
    return lax.dot_general(a, b, dims, preferred_element_type=jnp.float32)


def kernel(geo, slots_ref, corpus_ref, out_ref, spot, ids_src, send, send_ids, got, got_ids,
           summed, rows, cols, best, parts, s_send, s_recv, i_send, i_recv,
           r_send, r_recv, c_send, c_recv, p_send, p_recv):
    ti_count, tj_count, count, features, sub, cap, chunks = geo
    owners = 2 * tj_count
    xs = ti_count // CORES
    zs = tj_count // 2
    blk = sub * tj_count
    cluster = blk * ti_count
    step = sub // chunks
    g, ti, tj = lax.axis_index("grp"), lax.axis_index("ti"), lax.axis_index("tj")
    x, core = ti // CORES, ti % CORES
    zh, zl = tj // zs, tj % zs
    lin = g * tj_count + tj

    def dev(gg, tt, jj):
        return {"grp": gg, "ti": tt, "tj": jj}

    def owner_dev(k):
        d = lax.rem(lin + k, owners)
        return d, dev(d // tj_count, ti, lax.rem(d, tj_count))

    def row_dev(dx, dy):
        return dev(lax.rem(g + dy, 2), lax.rem(x + dx, xs) * CORES + core, tj)

    def col_dev(dc, dz):
        return dev(g, x * CORES + lax.rem(core + dc, CORES), zh * zs + lax.rem(zl + dz, zs))

    def final_dev(dx, dy):
        return dev(zh, lax.rem(x + dx, xs) * CORES + core, lax.rem(g + dy, 2) * zs + zl)

    def feeder_dev(dx, dy):
        return dev(dy, lax.rem(x + dx, xs) * CORES + core, g * zs + zl)

    barrier = pltpu.get_barrier_semaphore()
    greeted = 0
    targets = [owner_dev(k)[1] for k in range(1, owners)]
    targets += [row_dev(dx, dy) for dx in range(1, xs) for dy in range(2)]
    targets += [col_dev(dc, dz) for dc in range(1, CORES) for dz in range(zs)]
    targets += [final_dev(dx, dy) for dx in range(1, xs) for dy in range(2)]
    targets += [feeder_dev(dx, dy) for dx in range(1, xs) for dy in range(2)]
    for target in targets:
        pl.semaphore_signal(barrier, inc=1, device_id=target, device_id_type=MESH)
        greeted += 1

    v = slots_ref[...]
    member = v >= 0
    second = (v >= cluster).astype(jnp.int32)
    inblk = v - second * cluster - ti * blk
    s = jnp.zeros_like(v)
    for k in range(1, tj_count):
        s = s + (inblk >= k * sub).astype(jnp.int32)
    pos = inblk - s * sub
    s_hi = (s >= zs).astype(jnp.int32)
    owner = s_hi * tj_count + second * zs + s - s_hi * zs
    owner = jnp.where(member, owner, owners)
    piece = 256 if count % 256 == 0 else 128
    before = (
        lax.broadcasted_iota(jnp.int32, (piece, piece), 0)
        < lax.broadcasted_iota(jnp.int32, (piece, piece), 1)
    ).astype(jnp.bfloat16)
    carry = jnp.zeros((owners, 1), jnp.float32)
    owner_iota = lax.broadcasted_iota(jnp.int32, (owners, piece), 0)
    for p in range(count // piece):
        part = slice(p * piece, (p + 1) * piece)
        mine = owner_iota == owner[:, part]
        hot = mine.astype(jnp.float32)
        ranks = dot(hot.astype(jnp.bfloat16), before, NN) + carry
        carry = carry + jnp.sum(hot, axis=1, keepdims=True)
        rank = jnp.sum(jnp.where(mine, ranks, 0.0), axis=0, keepdims=True).astype(jnp.int32)
        spot[:, part] = jnp.where(member[:, part], owner[:, part] * cap + rank, owners * cap)
    line = lax.broadcasted_iota(jnp.int32, (16, count), 0)
    ids_src[...] = jnp.where(
        line == 0, pos >> 5, jnp.where(line == 1, pos & 31, (line == 2).astype(jnp.int32))
    ).astype(jnp.float32).astype(jnp.bfloat16)

    pl.semaphore_wait(barrier, greeted)

    def pack(k):
        d = lax.rem(lin + k, owners)
        pick = (
            spot[...] == d * cap + lax.broadcasted_iota(jnp.int32, (cap, count), 0)
        ).astype(jnp.float32).astype(jnp.bfloat16)
        packed = dot(pick, corpus_ref[0], NN).astype(jnp.bfloat16)
        ids = dot(ids_src[...], pick, NT).astype(jnp.bfloat16)
        return packed, ids

    def row_copy(k):
        return pltpu.make_async_remote_copy(
            send.at[k], got.at[k], s_send.at[k], s_recv.at[k],
            device_id=owner_dev(k)[1], device_id_type=MESH)

    def id_copy(k):
        return pltpu.make_async_remote_copy(
            send_ids.at[k], got_ids.at[k], i_send.at[k], i_recv.at[k],
            device_id=owner_dev(k)[1], device_id_type=MESH)

    def send_step(k, _):
        packed, ids = pack(k)
        send[k] = packed
        send_ids[k, :, :cap] = ids

        @pl.when(k > 1)
        def _():
            id_copy(k - 1).start()
            row_copy(k - 1).start()
        return 0

    lax.fori_loop(1, owners, send_step, 0)
    packed, ids = pack(0)
    got[0] = packed
    got_ids[0, :, :cap] = ids
    id_copy(owners - 1).start()
    row_copy(owners - 1).start()

    def place(k):
        line_ids = got_ids[k, :, :cap].astype(jnp.float32)
        where = (line_ids[0:1] * 32.0 + line_ids[1:2]).astype(jnp.int32)
        where = jnp.where(line_ids[2:3] > 0.5, where, sub)
        pick = (
            where == lax.broadcasted_iota(jnp.int32, (sub, cap), 0)
        ).astype(jnp.float32).astype(jnp.bfloat16)
        return dot(pick, got[k], NN)

    summed[...] = place(0)

    def place_step(k, _):
        id_copy(k).wait_recv()
        row_copy(k).wait_recv()
        summed[...] += place(k)
        return 0

    lax.fori_loop(1, owners, place_step, 0)

    row_peers = [(dx, dy) for dx in range(xs) for dy in range(2)]
    col_peers = [(dc, dz) for dc in range(CORES) for dz in range(zs)]
    row_slot = {peer: i for i, peer in enumerate(row_peers)}
    col_slot = {peer: i for i, peer in enumerate(col_peers)}

    def block_copy(peer, i, is_row):
        part = pl.ds(i * step, step)
        if is_row:
            slot = row_slot[((-peer[0]) % xs, (-peer[1]) % 2)]
            return pltpu.make_async_remote_copy(
                rows.at[0, part], rows.at[slot, part],
                r_send.at[slot, i], r_recv.at[slot, i],
                device_id=row_dev(*peer), device_id_type=MESH)
        slot = col_slot[((-peer[0]) % CORES, (-peer[1]) % zs)]
        return pltpu.make_async_remote_copy(
            cols.at[0, part], cols.at[slot, part],
            c_send.at[slot, i], c_recv.at[slot, i],
            device_id=col_dev(*peer), device_id_type=MESH)

    copies = []

    def launch(i):
        for peer in col_peers[1:]:
            copies.append(block_copy(peer, i, False))
            copies[-1].start()
        for peer in row_peers[1:]:
            copies.append(block_copy(peer, i, True))
            copies[-1].start()

    for i in range(chunks):
        part = slice(i * step, (i + 1) * step)
        wide = summed[part]
        squares = jnp.sum(wide * wide, axis=1, keepdims=True)
        unit = (wide * lax.rsqrt(squares + EPSILON)).astype(jnp.bfloat16)
        rows[0, part] = unit
        cols[0, part] = unit
        if i:
            launch(i - 1)

    best[...] = jnp.full(best.shape, -2.0, jnp.float32)
    launch(chunks - 1)

    def tile(row, i, col, own=False):
        part = pl.ds(pl.multiple_of(i * step, step), step)
        scores = dot(cols[col], rows[row, part, :], NT)
        if own:
            same = (
                lax.broadcasted_iota(jnp.int32, (sub, step), 0)
                == i * step + lax.broadcasted_iota(jnp.int32, (sub, step), 1)
            )
            scores = jnp.where(same, -2.0, scores)
        top = jnp.max(scores.reshape(sub // 8, 8, step), axis=0)
        best[row, i] = jnp.maximum(best[row, i], top)
        return 0

    lax.fori_loop(0, chunks, lambda i, _: tile(0, i, 0, True), 0)
    for col in range(1, len(col_peers)):
        for i in range(chunks):
            block_copy(((-col_peers[col][0]) % CORES, (-col_peers[col][1]) % zs), i, False).wait_recv()
        lax.fori_loop(0, chunks, lambda i, _, col=col: tile(0, i, col), 0)

    def part_copy(row):
        return pltpu.make_async_remote_copy(
            best.at[row], parts.at[x * 2 + g], p_send.at[row], p_recv.at[x * 2 + g],
            device_id=final_dev(*row_peers[row]), device_id_type=MESH)

    stays = zh == g

    @pl.when(stays)
    def _():
        parts[x * 2 + g] = best[0]

    @pl.when(jnp.logical_not(stays))
    def _():
        part_copy(0).start()

    for row in range(1, len(row_peers)):
        peer = row_peers[row]
        for i in range(chunks):
            block_copy(((-peer[0]) % xs, (-peer[1]) % 2), i, True).wait_recv()
            lax.fori_loop(0, len(col_peers), lambda col, _, row=row, i=i: tile(row, i, col), 0)
        part_copy(row).start()

    for feeder in range(len(row_peers)):
        arrived = pltpu.make_async_remote_copy(
            best.at[0], parts.at[feeder], p_send.at[0], p_recv.at[feeder],
            device_id=final_dev(0, 0), device_id_type=MESH)
        if feeder < len(row_peers):
            here = jnp.logical_and(stays, x * 2 + g == feeder)

            @pl.when(jnp.logical_not(here))
            def _(arrived=arrived):
                arrived.wait_recv()
    for i in range(chunks):
        top = jnp.max(parts[:, i], axis=0)
        out_ref[:, i * step : (i + 1) * step] = jnp.max(top, axis=0, keepdims=True)

    @pl.when(jnp.logical_not(stays))
    def _():
        part_copy(0).wait_send()

    for row in range(1, len(row_peers)):
        part_copy(row).wait_send()
    for copy in copies:
        copy.wait_send()

    def drain(k, _):
        id_copy(k).wait_send()
        row_copy(k).wait_send()
        return 0

    lax.fori_loop(1, owners, drain, 0)


def per_device(corpus, slot_of_row):
    ti_count, tj_count = lax.axis_size("ti"), lax.axis_size("tj")
    _, count, features = corpus.shape
    sub = count // 2
    cap = sub // tj_count
    owners = 2 * tj_count
    chunks = 3
    step = sub // chunks
    row_blocks, col_blocks = ti_count // CORES * 2, tj_count // 2 * CORES
    wide_cap = -(-cap // 128) * 128
    dma = pltpu.SemaphoreType.DMA
    vmem = pl.BlockSpec(memory_space=pltpu.VMEM)
    return pl.pallas_call(
        functools.partial(kernel, (ti_count, tj_count, count, features, sub, cap, chunks)),
        out_shape=jax.ShapeDtypeStruct((1, sub), jnp.float32),
        in_specs=[vmem, vmem],
        out_specs=vmem,
        scratch_shapes=[
            pltpu.VMEM((1, count), jnp.int32),
            pltpu.VMEM((16, count), jnp.bfloat16),
            pltpu.VMEM((owners, cap, features), jnp.bfloat16),
            pltpu.VMEM((owners, 16, wide_cap), jnp.bfloat16),
            pltpu.VMEM((owners, cap, features), jnp.bfloat16),
            pltpu.VMEM((owners, 16, wide_cap), jnp.bfloat16),
            pltpu.VMEM((sub, features), jnp.float32),
            pltpu.VMEM((row_blocks, sub, features), jnp.bfloat16),
            pltpu.VMEM((col_blocks, sub, features), jnp.bfloat16),
            pltpu.VMEM((row_blocks, chunks, 8, step), jnp.float32),
            pltpu.VMEM((row_blocks, chunks, 8, step), jnp.float32),
            dma((owners,)), dma((owners,)), dma((owners,)), dma((owners,)),
            dma((row_blocks, chunks)), dma((row_blocks, chunks)),
            dma((col_blocks, chunks)), dma((col_blocks, chunks)),
            dma((row_blocks,)), dma((row_blocks,)),
        ],
        compiler_params=pltpu.CompilerParams(
            collective_id=0, has_side_effects=True, vmem_limit_bytes=60 * 1024 * 1024),
    )(slot_of_row, corpus)


def solution(mesh):
    in_specs = (P("grp", ("ti", "tj"), None), P("grp", ("ti", "tj")))
    out_specs = P("grp", ("ti", "tj"))
    return jax.shard_map(
        per_device, mesh=mesh, in_specs=in_specs, out_specs=out_specs, check_vma=False
    )
```

```python
import functools

import jax
import jax.numpy as jnp
from jax import lax
from jax.experimental import pallas as pl
from jax.experimental.pallas import tpu as pltpu
from jax.sharding import PartitionSpec as P

MESH = pl.DeviceIdType.MESH
NT = (((1,), (1,)), ((), ()))
NN = (((1,), (0,)), ((), ()))
CORES = 2
EPSILON = 1e-06


def dot(a, b, dims):
    return lax.dot_general(a, b, dims, preferred_element_type=jnp.float32)


def kernel(geo, slots_ref, corpus_ref, out_ref, spot, ids_src, send, send_ids, got, got_ids,
           picks, summed, raw, units, best, parts, s_send, s_recv, i_send, i_recv,
           b_send, b_recv, p_send, p_recv):
    ti_count, tj_count, count, features, sub, cap, chunks, parts_f = geo
    width = features // parts_f
    owners = 2 * tj_count
    xs = ti_count // CORES
    zs = tj_count // 2
    blk = sub * tj_count
    cluster = blk * ti_count
    step = sub // chunks
    g, ti, tj = lax.axis_index("grp"), lax.axis_index("ti"), lax.axis_index("tj")
    x, core = ti // CORES, ti % CORES
    zh, zl = tj // zs, tj % zs
    lin = g * tj_count + tj

    def dev(gg, tt, jj):
        return {"grp": gg, "ti": tt, "tj": jj}

    def owner_dev(k):
        d = lax.rem(lin + k, owners)
        return d, dev(d // tj_count, ti, lax.rem(d, tj_count))

    def row_dev(dx, dy):
        return dev(lax.rem(g + dy, 2), lax.rem(x + dx, xs) * CORES + core, tj)

    def col_dev(dc, dz):
        return dev(g, x * CORES + lax.rem(core + dc, CORES), zh * zs + lax.rem(zl + dz, zs))

    def final_dev(dx, dy):
        return dev(zh, lax.rem(x + dx, xs) * CORES + core, lax.rem(g + dy, 2) * zs + zl)

    def feeder_dev(dx, dy):
        return dev(dy, lax.rem(x + dx, xs) * CORES + core, g * zs + zl)

    barrier = pltpu.get_barrier_semaphore()
    greeted = 0
    targets = [owner_dev(k)[1] for k in range(1, owners)]
    targets += [row_dev(dx, dy) for dx in range(1, xs) for dy in range(2)]
    targets += [col_dev(dc, dz) for dc in range(1, CORES) for dz in range(zs)]
    targets += [final_dev(dx, dy) for dx in range(1, xs) for dy in range(2)]
    targets += [feeder_dev(dx, dy) for dx in range(1, xs) for dy in range(2)]
    for target in targets:
        pl.semaphore_signal(barrier, inc=1, device_id=target, device_id_type=MESH)
        greeted += 1

    v = slots_ref[...]
    member = v >= 0
    second = (v >= cluster).astype(jnp.int32)
    inblk = v - second * cluster - ti * blk
    s = jnp.zeros_like(v)
    for k in range(1, tj_count):
        s = s + (inblk >= k * sub).astype(jnp.int32)
    pos = inblk - s * sub
    s_hi = (s >= zs).astype(jnp.int32)
    owner = s_hi * tj_count + second * zs + s - s_hi * zs
    owner = jnp.where(member, owner, owners)
    piece = 256 if count % 256 == 0 else 128
    before = (
        lax.broadcasted_iota(jnp.int32, (piece, piece), 0)
        < lax.broadcasted_iota(jnp.int32, (piece, piece), 1)
    ).astype(jnp.bfloat16)
    carry = jnp.zeros((owners, 1), jnp.float32)
    owner_iota = lax.broadcasted_iota(jnp.int32, (owners, piece), 0)
    for p in range(count // piece):
        part = slice(p * piece, (p + 1) * piece)
        mine = owner_iota == owner[:, part]
        hot = mine.astype(jnp.float32)
        ranks = dot(hot.astype(jnp.bfloat16), before, NN) + carry
        carry = carry + jnp.sum(hot, axis=1, keepdims=True)
        rank = jnp.sum(jnp.where(mine, ranks, 0.0), axis=0, keepdims=True).astype(jnp.int32)
        spot[:, part] = jnp.where(member[:, part], owner[:, part] * cap + rank, owners * cap)
    line = lax.broadcasted_iota(jnp.int32, (16, count), 0)
    ids_src[...] = jnp.where(
        line == 0, pos >> 5, jnp.where(line == 1, pos & 31, (line == 2).astype(jnp.int32))
    ).astype(jnp.float32).astype(jnp.bfloat16)

    row_peers = [(dx, dy) for dx in range(xs) for dy in range(2)]
    col_peers = [(dc, dz) for dc in range(CORES) for dz in range(zs)]
    own = len(row_peers) - 1
    row_at = {peer: i - 1 if i else own for i, peer in enumerate(row_peers)}
    col_at = {peer: own + i for i, peer in enumerate(col_peers)}
    lanes = [pl.ds(f * width, width) for f in range(parts_f)]
    half = sub // 2

    def pick_of(k):
        d = lax.rem(lin + k, owners)
        return (
            spot[...] == d * cap + lax.broadcasted_iota(jnp.int32, (cap, count), 0)
        ).astype(jnp.float32).astype(jnp.bfloat16)

    def row_copy(k, f):
        return pltpu.make_async_remote_copy(
            send.at[k, :, lanes[f]], got.at[k, :, lanes[f]], s_send.at[k, f], s_recv.at[k, f],
            device_id=owner_dev(k)[1], device_id_type=MESH)

    def id_copy(k):
        return pltpu.make_async_remote_copy(
            send_ids.at[k], got_ids.at[k], i_send.at[k], i_recv.at[k],
            device_id=owner_dev(k)[1], device_id_type=MESH)

    def start_pair(k, f):
        if f == 0:
            id_copy(k).start()
        row_copy(k, f).start()

    def pack(f):
        def one(k, _):
            pick = pick_of(k)
            send[k, :, lanes[f]] = dot(pick, corpus_ref[0, :, lanes[f]], NN).astype(jnp.bfloat16)
            if f == 0:
                send_ids[k, :, :cap] = dot(ids_src[...], pick, NT).astype(jnp.bfloat16)

            @pl.when(k > 1)
            def _():
                start_pair(k - 1, f)
            return 0

        lax.fori_loop(1, owners, one, 0)
        pick = pick_of(0)
        got[0, :, lanes[f]] = dot(pick, corpus_ref[0, :, lanes[f]], NN).astype(jnp.bfloat16)
        if f == 0:
            got_ids[0, :, :cap] = dot(ids_src[...], pick, NT).astype(jnp.bfloat16)
        start_pair(owners - 1, f)

    def place(f):
        def one(k, first):
            if f == 0:
                line_ids = got_ids[k, :, :cap].astype(jnp.float32)
                where = (line_ids[0:1] * 32.0 + line_ids[1:2]).astype(jnp.int32)
                where = jnp.where(line_ids[2:3] > 0.5, where, sub)
                picks[k] = (
                    where == lax.broadcasted_iota(jnp.int32, (sub, cap), 0)
                ).astype(jnp.float32).astype(jnp.bfloat16)
            term = dot(picks[k], got[k, :, lanes[f]], NN)
            summed[...] = term if first else summed[...] + term

        def arrived(k, _):
            if f == 0:
                id_copy(k).wait_recv()
            row_copy(k, f).wait_recv()
            one(k, False)
            return 0

        one(0, True)
        lax.fori_loop(1, owners, arrived, 0)

    started, waited = [], set()

    def block_copy(source, target, f, h, device):
        area = (pl.ds(h * half, half), lanes[f])
        return pltpu.make_async_remote_copy(
            raw.at[(source,) + area], raw.at[(target,) + area],
            b_send.at[target, f, h], b_recv.at[target, f, h],
            device_id=device, device_id_type=MESH)

    def ship(source, target, f, h, device):
        copy = block_copy(source, target, f, h, device)
        copy.start()
        started.append(copy)

    def need(block, f, h):
        if (block, f, h) not in waited:
            waited.add((block, f, h))
            block_copy(own, block, f, h, row_dev(0, 1)).wait_recv()

    def launch(f):
        for n in range(2):
            for dx, dy in row_peers[1:]:
                if xs == 2 and dx and dy:
                    continue
                ship(own, row_at[(-dx) % xs, (-dy) % 2], f, 1 - n if dy else n, row_dev(dx, dy))
            for dc, dz in col_peers[1:]:
                if zs == 2 and dc and dz:
                    continue
                ship(own, col_at[(-dc) % CORES, (-dz) % zs], f, n, col_dev(dc, dz))

    def relay(f):
        if xs == 2:
            need(row_at[1, 0], f, 0)
            ship(row_at[1, 0], row_at[1, 1], f, 0, row_dev(0, 1))
            need(row_at[0, 1], f, 1)
            ship(row_at[0, 1], row_at[1, 1], f, 1, row_dev(1, 0))
        if zs == 2:
            for h in range(2):
                need(col_at[0, 1], f, h)
                ship(col_at[0, 1], col_at[1, 1], f, h, col_dev(1, 0))

    pl.semaphore_wait(barrier, greeted)
    ahead = 2
    for f in range(min(ahead, parts_f)):
        pack(f)
    for f in range(parts_f):
        place(f)
        raw[own, :, lanes[f]] = summed[...].astype(jnp.bfloat16)
        if f == 0:
            best[...] = jnp.full(best.shape, -2.0, jnp.float32)
        if f:
            relay(f - 1)
        launch(f)
        if f + ahead < parts_f:
            pack(f + ahead)

    def norm(block):
        for f in range(parts_f):
            for h in range(2):
                if block != own:
                    need(block, f, h)

        def one(n, _):
            area = pl.ds(pl.multiple_of(n * 128, 128), 128)
            wide = raw[block, area, :].astype(jnp.float32)
            squares = jnp.sum(wide * wide, axis=1, keepdims=True)
            units[block, area, :] = (wide * lax.rsqrt(squares + EPSILON)).astype(jnp.bfloat16)
            return 0

        lax.fori_loop(0, sub // 128, one, 0)

    def tile(row, i, col, diagonal=False):
        part = pl.ds(pl.multiple_of(i * step, step), step)
        scores = dot(units[own + col], units[row, part, :], NT)
        if diagonal:
            same = (
                lax.broadcasted_iota(jnp.int32, (sub, step), 0)
                == i * step + lax.broadcasted_iota(jnp.int32, (sub, step), 1)
            )
            scores = jnp.where(same, -2.0, scores)
        top = jnp.max(scores.reshape(sub // 8, 8, step), axis=0)
        best[row, i] = jnp.maximum(best[row, i], top)
        return 0

    norm(own)
    lax.fori_loop(0, chunks, lambda i, _: tile(own, i, 0, True), 0)
    relay(parts_f - 1)
    for col in range(1, len(col_peers)):
        norm(own + col)
        lax.fori_loop(0, chunks, lambda i, _, col=col: tile(own, i, col), 0)

    def part_copy(peer):
        return pltpu.make_async_remote_copy(
            best.at[row_at[peer]], parts.at[x * 2 + g],
            p_send.at[row_at[peer]], p_recv.at[x * 2 + g],
            device_id=final_dev(*peer), device_id_type=MESH)

    stays = zh == g

    @pl.when(stays)
    def _():
        parts[x * 2 + g] = best[own]

    @pl.when(jnp.logical_not(stays))
    def _():
        part_copy((0, 0)).start()

    order = [peer for peer in row_peers[1:] if not (peer[0] and peer[1])]
    order += [peer for peer in row_peers[1:] if peer[0] and peer[1]]
    total = chunks * len(col_peers)
    for peer in order:
        row = row_at[peer]
        norm(row)
        lax.fori_loop(
            0, total, lambda n, _, row=row: tile(row, n // len(col_peers), n % len(col_peers)), 0)
        part_copy(peer).start()

    for feeder in range(len(row_peers)):
        arrived = pltpu.make_async_remote_copy(
            best.at[0], parts.at[feeder], p_send.at[0], p_recv.at[feeder],
            device_id=row_dev(0, 1), device_id_type=MESH)
        here = jnp.logical_and(stays, x * 2 + g == feeder)

        @pl.when(jnp.logical_not(here))
        def _(arrived=arrived):
            arrived.wait_recv()
    for i in range(chunks):
        top = jnp.max(parts[:, i], axis=0)
        out_ref[:, i * step : (i + 1) * step] = jnp.max(top, axis=0, keepdims=True)

    @pl.when(jnp.logical_not(stays))
    def _():
        part_copy((0, 0)).wait_send()

    for peer in row_peers[1:]:
        part_copy(peer).wait_send()
    for copy in started:
        copy.wait_send()

    def drain(k, _):
        id_copy(k).wait_send()
        for f in range(parts_f):
            row_copy(k, f).wait_send()
        return 0

    lax.fori_loop(1, owners, drain, 0)


def per_device(corpus, slot_of_row):
    ti_count, tj_count = lax.axis_size("ti"), lax.axis_size("tj")
    _, count, features = corpus.shape
    sub = count // 2
    cap = sub // tj_count
    owners = 2 * tj_count
    chunks, parts_f = 3, 4
    step = sub // chunks
    row_blocks, col_blocks = ti_count // CORES * 2, tj_count // 2 * CORES
    blocks = row_blocks + col_blocks - 1
    wide_cap = -(-cap // 128) * 128
    dma = pltpu.SemaphoreType.DMA
    vmem = pl.BlockSpec(memory_space=pltpu.VMEM)
    return pl.pallas_call(
        functools.partial(kernel, (ti_count, tj_count, count, features, sub, cap, chunks, parts_f)),
        out_shape=jax.ShapeDtypeStruct((1, sub), jnp.float32),
        in_specs=[vmem, vmem],
        out_specs=vmem,
        scratch_shapes=[
            pltpu.VMEM((1, count), jnp.int32),
            pltpu.VMEM((16, count), jnp.bfloat16),
            pltpu.VMEM((owners, cap, features), jnp.bfloat16),
            pltpu.VMEM((owners, 16, wide_cap), jnp.bfloat16),
            pltpu.VMEM((owners, cap, features), jnp.bfloat16),
            pltpu.VMEM((owners, 16, wide_cap), jnp.bfloat16),
            pltpu.VMEM((owners, sub, cap), jnp.bfloat16),
            pltpu.VMEM((sub, features // parts_f), jnp.float32),
            pltpu.VMEM((blocks, sub, features), jnp.bfloat16),
            pltpu.VMEM((blocks, sub, features), jnp.bfloat16),
            pltpu.VMEM((row_blocks, chunks, 8, step), jnp.float32),
            pltpu.VMEM((row_blocks, chunks, 8, step), jnp.float32),
            dma((owners, parts_f)), dma((owners, parts_f)), dma((owners,)), dma((owners,)),
            dma((blocks, parts_f, 2)), dma((blocks, parts_f, 2)),
            dma((row_blocks,)), dma((row_blocks,)),
        ],
        compiler_params=pltpu.CompilerParams(
            collective_id=0, has_side_effects=True, vmem_limit_bytes=60 * 1024 * 1024),
    )(slot_of_row, corpus)


def solution(mesh):
    in_specs = (P("grp", ("ti", "tj"), None), P("grp", ("ti", "tj")))
    out_specs = P("grp", ("ti", "tj"))
    return jax.shard_map(
        per_device, mesh=mesh, in_specs=in_specs, out_specs=out_specs, check_vma=False
    )
```

```python
import functools

import jax
import jax.numpy as jnp
from jax import lax
from jax.experimental import pallas as pl
from jax.experimental.pallas import tpu as pltpu
from jax.sharding import PartitionSpec as P

MESH = pl.DeviceIdType.MESH
NT = (((1,), (1,)), ((), ()))
NN = (((1,), (0,)), ((), ()))
CORES = 2
EPSILON = 1e-06


def dot(a, b, dims):
    return lax.dot_general(a, b, dims, preferred_element_type=jnp.float32)


def kernel(geo, slots_ref, corpus_ref, out_ref, spot, ids_src, send, send_ids, got, got_ids,
           picks, summed, raw, units, best, parts, s_send, s_recv, i_send, i_recv,
           b_send, b_recv, p_send, p_recv):
    ti_count, tj_count, count, features, sub, cap, chunks, parts_f = geo
    width = features // parts_f
    owners = 2 * tj_count
    xs = ti_count // CORES
    zs = tj_count // 2
    blk = sub * tj_count
    cluster = blk * ti_count
    step = sub // chunks
    g, ti, tj = lax.axis_index("grp"), lax.axis_index("ti"), lax.axis_index("tj")
    x, core = ti // CORES, ti % CORES
    zh, zl = tj // zs, tj % zs
    lin = g * tj_count + tj

    def dev(gg, tt, jj):
        return {"grp": gg, "ti": tt, "tj": jj}

    def owner_dev(k):
        d = lax.rem(lin + k, owners)
        return d, dev(d // tj_count, ti, lax.rem(d, tj_count))

    def row_dev(dx, dy):
        return dev(lax.rem(g + dy, 2), lax.rem(x + dx, xs) * CORES + core, tj)

    def col_dev(dc, dz):
        return dev(g, x * CORES + lax.rem(core + dc, CORES), zh * zs + lax.rem(zl + dz, zs))

    def final_dev(dx, dy):
        return dev(zh, lax.rem(x + dx, xs) * CORES + core, lax.rem(g + dy, 2) * zs + zl)

    def feeder_dev(dx, dy):
        return dev(dy, lax.rem(x + dx, xs) * CORES + core, g * zs + zl)

    barrier = pltpu.get_barrier_semaphore()
    greeted = 0
    targets = [owner_dev(k)[1] for k in range(1, owners)]
    targets += [row_dev(dx, dy) for dx in range(1, xs) for dy in range(2)]
    targets += [col_dev(dc, dz) for dc in range(1, CORES) for dz in range(zs)]
    targets += [final_dev(dx, dy) for dx in range(1, xs) for dy in range(2)]
    targets += [feeder_dev(dx, dy) for dx in range(1, xs) for dy in range(2)]
    for target in targets:
        pl.semaphore_signal(barrier, inc=1, device_id=target, device_id_type=MESH)
        greeted += 1

    v = slots_ref[...]
    member = v >= 0
    second = (v >= cluster).astype(jnp.int32)
    inblk = v - second * cluster - ti * blk
    s = jnp.zeros_like(v)
    for k in range(1, tj_count):
        s = s + (inblk >= k * sub).astype(jnp.int32)
    pos = inblk - s * sub
    s_hi = (s >= zs).astype(jnp.int32)
    owner = s_hi * tj_count + second * zs + s - s_hi * zs
    owner = jnp.where(member, owner, owners)
    piece = 256 if count % 256 == 0 else 128
    before = (
        lax.broadcasted_iota(jnp.int32, (piece, piece), 0)
        < lax.broadcasted_iota(jnp.int32, (piece, piece), 1)
    ).astype(jnp.bfloat16)
    carry = jnp.zeros((owners, 1), jnp.float32)
    owner_iota = lax.broadcasted_iota(jnp.int32, (owners, piece), 0)
    for p in range(count // piece):
        part = slice(p * piece, (p + 1) * piece)
        mine = owner_iota == owner[:, part]
        hot = mine.astype(jnp.float32)
        ranks = dot(hot.astype(jnp.bfloat16), before, NN) + carry
        carry = carry + jnp.sum(hot, axis=1, keepdims=True)
        rank = jnp.sum(jnp.where(mine, ranks, 0.0), axis=0, keepdims=True).astype(jnp.int32)
        spot[:, part] = jnp.where(member[:, part], owner[:, part] * cap + rank, owners * cap)
    line = lax.broadcasted_iota(jnp.int32, (16, count), 0)
    ids_src[...] = jnp.where(
        line == 0, pos >> 5, jnp.where(line == 1, pos & 31, (line == 2).astype(jnp.int32))
    ).astype(jnp.float32).astype(jnp.bfloat16)

    row_peers = [(dx, dy) for dx in range(xs) for dy in range(2)]
    col_peers = [(dc, dz) for dc in range(CORES) for dz in range(zs)]
    own = len(row_peers) - 1
    row_at = {peer: i - 1 if i else own for i, peer in enumerate(row_peers)}
    col_at = {peer: own + i for i, peer in enumerate(col_peers)}
    lanes = [pl.ds(f * width, width) for f in range(parts_f)]
    half = sub // 2

    def pick_of(k):
        d = lax.rem(lin + k, owners)
        return (
            spot[...] == d * cap + lax.broadcasted_iota(jnp.int32, (cap, count), 0)
        ).astype(jnp.float32).astype(jnp.bfloat16)

    def row_copy(k, f):
        return pltpu.make_async_remote_copy(
            send.at[k, :, lanes[f]], got.at[k, :, lanes[f]], s_send.at[k, f], s_recv.at[k, f],
            device_id=owner_dev(k)[1], device_id_type=MESH)

    def id_copy(k):
        return pltpu.make_async_remote_copy(
            send_ids.at[k], got_ids.at[k], i_send.at[k], i_recv.at[k],
            device_id=owner_dev(k)[1], device_id_type=MESH)

    def start_pair(k, f):
        if f == 0:
            id_copy(k).start()
        row_copy(k, f).start()

    def pack(f):
        def one(k, _):
            pick = pick_of(k)
            send[k, :, lanes[f]] = dot(pick, corpus_ref[0, :, lanes[f]], NN).astype(jnp.bfloat16)
            if f == 0:
                send_ids[k, :, :cap] = dot(ids_src[...], pick, NT).astype(jnp.bfloat16)

            @pl.when(k > 1)
            def _():
                start_pair(k - 1, f)
            return 0

        lax.fori_loop(1, owners, one, 0)
        pick = pick_of(0)
        got[0, :, lanes[f]] = dot(pick, corpus_ref[0, :, lanes[f]], NN).astype(jnp.bfloat16)
        if f == 0:
            got_ids[0, :, :cap] = dot(ids_src[...], pick, NT).astype(jnp.bfloat16)
        start_pair(owners - 1, f)

    def place(f):
        def one(k, first):
            if f == 0:
                line_ids = got_ids[k, :, :cap].astype(jnp.float32)
                where = (line_ids[0:1] * 32.0 + line_ids[1:2]).astype(jnp.int32)
                where = jnp.where(line_ids[2:3] > 0.5, where, sub)
                picks[k] = (
                    where == lax.broadcasted_iota(jnp.int32, (sub, cap), 0)
                ).astype(jnp.float32).astype(jnp.bfloat16)
            term = dot(picks[k], got[k, :, lanes[f]], NN)
            summed[...] = term if first else summed[...] + term

        def arrived(k, _):
            if f == 0:
                id_copy(k).wait_recv()
            row_copy(k, f).wait_recv()
            one(k, False)
            return 0

        one(0, True)
        lax.fori_loop(1, owners, arrived, 0)

    started, waited = [], set()

    def block_copy(source, target, f, h, device):
        area = (pl.ds(h * half, half), lanes[f])
        return pltpu.make_async_remote_copy(
            raw.at[(source,) + area], raw.at[(target,) + area],
            b_send.at[target, f, h], b_recv.at[target, f, h],
            device_id=device, device_id_type=MESH)

    def ship(source, target, f, h, device):
        copy = block_copy(source, target, f, h, device)
        copy.start()
        started.append(copy)

    def need(block, f, h):
        if (block, f, h) not in waited:
            waited.add((block, f, h))
            block_copy(own, block, f, h, row_dev(0, 1)).wait_recv()

    def launch(f):
        for n in range(2):
            for dx, dy in row_peers[1:]:
                if xs == 2 and dx and dy:
                    continue
                ship(own, row_at[(-dx) % xs, (-dy) % 2], f, 1 - n if dy else n, row_dev(dx, dy))
            for dc, dz in col_peers[1:]:
                if zs == 2 and dc and dz:
                    continue
                ship(own, col_at[(-dc) % CORES, (-dz) % zs], f, n, col_dev(dc, dz))

    def relay(f):
        if xs == 2:
            need(row_at[1, 0], f, 0)
            ship(row_at[1, 0], row_at[1, 1], f, 0, row_dev(0, 1))
            need(row_at[0, 1], f, 1)
            ship(row_at[0, 1], row_at[1, 1], f, 1, row_dev(1, 0))
        if zs == 2:
            for h in range(2):
                need(col_at[0, 1], f, h)
                ship(col_at[0, 1], col_at[1, 1], f, h, col_dev(1, 0))

    pl.semaphore_wait(barrier, greeted)
    ahead = 2
    for f in range(min(ahead, parts_f)):
        pack(f)
    for f in range(parts_f):
        place(f)
        raw[own, :, lanes[f]] = summed[...].astype(jnp.bfloat16)
        if f == 0:
            best[...] = jnp.full(best.shape, -2.0, jnp.float32)
        if f:
            relay(f - 1)
        launch(f)
        if f + ahead < parts_f:
            pack(f + ahead)

    def norm(block):
        for f in range(parts_f):
            for h in range(2):
                if block != own:
                    need(block, f, h)

        def one(n, _):
            area = pl.ds(pl.multiple_of(n * 128, 128), 128)
            wide = raw[block, area, :].astype(jnp.float32)
            squares = jnp.sum(wide * wide, axis=1, keepdims=True)
            units[block, area, :] = (wide * lax.rsqrt(squares + EPSILON)).astype(jnp.bfloat16)
            return 0

        lax.fori_loop(0, sub // 128, one, 0)

    def tile(row, i, col, diagonal=False):
        part = pl.ds(pl.multiple_of(i * step, step), step)
        scores = dot(units[own + col], units[row, part, :], NT)
        if diagonal:
            same = (
                lax.broadcasted_iota(jnp.int32, (sub, step), 0)
                == i * step + lax.broadcasted_iota(jnp.int32, (sub, step), 1)
            )
            scores = jnp.where(same, -2.0, scores)
        top = jnp.max(scores.reshape(sub // 8, 8, step), axis=0)
        best[row, i] = jnp.maximum(best[row, i], top)
        return 0

    norm(own)
    lax.fori_loop(0, chunks, lambda i, _: tile(own, i, 0, True), 0)
    relay(parts_f - 1)
    for col in range(1, len(col_peers)):
        norm(own + col)
        lax.fori_loop(0, chunks, lambda i, _, col=col: tile(own, i, col), 0)

    def part_copy(peer):
        return pltpu.make_async_remote_copy(
            best.at[row_at[peer]], parts.at[x * 2 + g],
            p_send.at[row_at[peer]], p_recv.at[x * 2 + g],
            device_id=final_dev(*peer), device_id_type=MESH)

    stays = zh == g

    @pl.when(stays)
    def _():
        parts[x * 2 + g] = best[own]

    @pl.when(jnp.logical_not(stays))
    def _():
        part_copy((0, 0)).start()

    order = [peer for peer in row_peers[1:] if not (peer[0] and peer[1])]
    order += [peer for peer in row_peers[1:] if peer[0] and peer[1]]
    total = chunks * len(col_peers)
    for peer in order:
        row = row_at[peer]
        norm(row)
        lax.fori_loop(
            0, total, lambda n, _, row=row: tile(row, n // len(col_peers), n % len(col_peers)), 0)
        part_copy(peer).start()

    for feeder in range(len(row_peers)):
        arrived = pltpu.make_async_remote_copy(
            best.at[0], parts.at[feeder], p_send.at[0], p_recv.at[feeder],
            device_id=row_dev(0, 1), device_id_type=MESH)
        here = jnp.logical_and(stays, x * 2 + g == feeder)

        @pl.when(jnp.logical_not(here))
        def _(arrived=arrived):
            arrived.wait_recv()
    for i in range(chunks):
        top = jnp.max(parts[:, i], axis=0)
        out_ref[:, i * step : (i + 1) * step] = jnp.max(top, axis=0, keepdims=True)

    @pl.when(jnp.logical_not(stays))
    def _():
        part_copy((0, 0)).wait_send()

    for peer in row_peers[1:]:
        part_copy(peer).wait_send()
    for copy in started:
        copy.wait_send()

    def drain(k, _):
        id_copy(k).wait_send()
        for f in range(parts_f):
            row_copy(k, f).wait_send()
        return 0

    lax.fori_loop(1, owners, drain, 0)


def per_device(corpus, slot_of_row):
    ti_count, tj_count = lax.axis_size("ti"), lax.axis_size("tj")
    _, count, features = corpus.shape
    sub = count // 2
    cap = sub // tj_count
    owners = 2 * tj_count
    chunks, parts_f = 1, 4
    step = sub // chunks
    row_blocks, col_blocks = ti_count // CORES * 2, tj_count // 2 * CORES
    blocks = row_blocks + col_blocks - 1
    wide_cap = -(-cap // 128) * 128
    dma = pltpu.SemaphoreType.DMA
    vmem = pl.BlockSpec(memory_space=pltpu.VMEM)
    return pl.pallas_call(
        functools.partial(kernel, (ti_count, tj_count, count, features, sub, cap, chunks, parts_f)),
        out_shape=jax.ShapeDtypeStruct((1, sub), jnp.float32),
        in_specs=[vmem, vmem],
        out_specs=vmem,
        scratch_shapes=[
            pltpu.VMEM((1, count), jnp.int32),
            pltpu.VMEM((16, count), jnp.bfloat16),
            pltpu.VMEM((owners, cap, features), jnp.bfloat16),
            pltpu.VMEM((owners, 16, wide_cap), jnp.bfloat16),
            pltpu.VMEM((owners, cap, features), jnp.bfloat16),
            pltpu.VMEM((owners, 16, wide_cap), jnp.bfloat16),
            pltpu.VMEM((owners, sub, cap), jnp.bfloat16),
            pltpu.VMEM((sub, features // parts_f), jnp.float32),
            pltpu.VMEM((blocks, sub, features), jnp.bfloat16),
            pltpu.VMEM((blocks, sub, features), jnp.bfloat16),
            pltpu.VMEM((row_blocks, chunks, 8, step), jnp.float32),
            pltpu.VMEM((row_blocks, chunks, 8, step), jnp.float32),
            dma((owners, parts_f)), dma((owners, parts_f)), dma((owners,)), dma((owners,)),
            dma((blocks, parts_f, 2)), dma((blocks, parts_f, 2)),
            dma((row_blocks,)), dma((row_blocks,)),
        ],
        compiler_params=pltpu.CompilerParams(
            collective_id=0, has_side_effects=True, vmem_limit_bytes=60 * 1024 * 1024),
    )(slot_of_row, corpus)


def solution(mesh):
    in_specs = (P("grp", ("ti", "tj"), None), P("grp", ("ti", "tj")))
    out_specs = P("grp", ("ti", "tj"))
    return jax.shard_map(
        per_device, mesh=mesh, in_specs=in_specs, out_specs=out_specs, check_vma=False
    )
```
